256 devices in a mesh: pipe: 16 (over z, core), tensor: 16 (over y, x).
Axes of the slice: x: 4, y: 4, z: 8, core: 2. Of those that a mesh axis runs over, the one named last changes fastest.
Arguments:
- handed_acts: bfloat16 [16, 256, 12288], P('pipe', None, 'tensor'), may hold values from -6 to 6
- handed_grads: bfloat16 [16, 256, 12288], P('pipe', None, 'tensor'), may hold values from -6 to 6
- saved_inputs: bfloat16 [16, 256, 12288], P('pipe', None, 'tensor'), may hold values from -6 to 6
- embedded: bfloat16 [256, 12288], P(None, 'tensor'), may hold values from -6 to 6
- loss_grad: bfloat16 [256, 12288], P(None, 'tensor'), may hold values from -6 to 6
- w_in: bfloat16 [16, 96, 3, 256, 256], P('pipe', 'tensor'), may hold values from -0.21875 to 0.21875
- w_out: bfloat16 [16, 96, 3, 256, 256], P('pipe', 'tensor'), may hold values from -0.15625 to 0.15625
- cols_in: int32 [96, 3], P('tensor'), may hold values from 0 to 2
- cols_out: int32 [96, 3], P('tensor'), may hold values from 0 to 2
Outputs:
- out_acts: bfloat16 [16, 256, 12288], P('pipe', None, 'tensor')
- in_grads: bfloat16 [16, 256, 12288], P('pipe', None, 'tensor')
- grad_w_in: bfloat16 [16, 96, 3, 256, 256], P('pipe', 'tensor')
- grad_w_out: bfloat16 [16, 96, 3, 256, 256], P('pipe', 'tensor')
The draws below stay inside these ranges and needn't reach their ends.
All inputs are finite; a program needn't handle non-finite values.
Results may differ from the reference program's by a relative error of at most 0.0049.
Values may be sent and summed in bfloat16 or wider, within the bound.
No kernel may reach another device: no remote copies, remote signals or barrier semaphores. Data moves between devices by JAX's collectives and lax.ppermute only.
A program may use at most 128 MiB of HBM per device.

```python
import jax
import jax.numpy as jnp
from jax import lax

D = 12288
FF = 24576
BLOCK = 256
SLOTS = 3
TOK = 256
SECTIONS = 16
DBLOCKS = 48
HBLOCKS = 96
FB_DEV = 3
HB_DEV = 6
N_TENSOR = 16


def touch_ends(result, rng, low, top_value):
    dims = result.shape
    spot = [jax.random.randint(jax.random.fold_in(rng, axis), (), 0, dims[axis]) for axis in range(len(dims))]
    result = result.at[tuple(spot)].set(low)
    longest = dims.index(max(dims))
    spot[longest] = (spot[longest] + 1) % dims[longest]
    return result.at[tuple(spot)].set(top_value)


def block_scale(rng, dims, split, least, largest):
    def one(position, blocks):
        steps = jax.random.uniform(jax.random.fold_in(jax.random.fold_in(rng, 6), position), (blocks,), jnp.float32, least / len(split), largest / len(split))
        return jnp.repeat(jnp.exp(steps), dims[position] // blocks).reshape((-1,) + (1,) * (len(dims) - position - 1))

    factor_of = one(*split[0])
    for cut in split[1:]:
        factor_of = factor_of * one(*cut)
    return factor_of


def scatter_about(stream_key, extent, width, limit, shards=(), held_as=jnp.bfloat16):
    loudness = block_scale(stream_key, extent, shards, -0.22, 0.18) if shards else 1.0
    values = jax.random.normal(stream_key, extent, jnp.float32) * width * loudness
    return jnp.minimum(jnp.maximum(values, -limit), limit).astype(held_as)


def setup_inputs(seed: int = 0) -> dict:
    keys = jax.random.split(jax.random.key(seed), 10)
    return {
        "handed_acts": scatter_about(keys[0], (SECTIONS, TOK, D), 1.0, 6.0, ((0, 16), (2, 16))),
        "handed_grads": scatter_about(keys[1], (SECTIONS, TOK, D), 1.0, 6.0, ((0, 16), (2, 16))),
        "saved_inputs": scatter_about(keys[2], (SECTIONS, TOK, D), 1.0, 6.0, ((0, 16), (2, 16))),
        "embedded": scatter_about(keys[3], (TOK, D), 1.0, 6.0, ((1, 16),)),
        "loss_grad": scatter_about(keys[4], (TOK, D), 1.0, 6.0, ((1, 16),)),
        "w_in": scatter_about(keys[5], (SECTIONS, HBLOCKS, SLOTS, BLOCK, BLOCK), (SLOTS * BLOCK) ** -0.5, 0.21875, ((0, 16), (1, 16))),
        "w_out": scatter_about(keys[6], (SECTIONS, HBLOCKS, SLOTS, BLOCK, BLOCK), (SLOTS * BLOCK * FF // D) ** -0.5, 0.15625, ((0, 16), (1, 16))),
        "cols_in": touch_ends(jax.random.randint(keys[7], (HBLOCKS, SLOTS), 0, FB_DEV), jax.random.fold_in(keys[7], 1), 0, FB_DEV - 1).astype(jnp.int32),
        "cols_out": touch_ends(jax.random.randint(keys[8], (HBLOCKS, SLOTS), 0, FB_DEV), jax.random.fold_in(keys[8], 1), 0, FB_DEV - 1).astype(jnp.int32),
    }


def smooth_gate(values):
    return jax.nn.gelu(values, approximate=True)

def block_targets(index_table):
    owners = jnp.arange(HBLOCKS, dtype=jnp.int32) // HB_DEV
    level_masks = jnp.array([0, 1, N_TENSOR // 2], dtype=jnp.int32)
    partners = jnp.bitwise_xor(owners[:, None], level_masks[None, :])
    return (partners * FB_DEV + index_table.astype(jnp.int32)).astype(jnp.int32)

def section_pass(forward_in, backward_in, out_grad, weight_in, weight_out, source_in, target_out):
    weight_in_wide = weight_in.astype(jnp.float32)
    weight_out_wide = weight_out.astype(jnp.float32)
    picked_fwd = forward_in.reshape(TOK, DBLOCKS, BLOCK)[:, source_in]
    pre_fwd = jnp.einsum('thkc,hkcd->thd', picked_fwd.astype(jnp.float32), weight_in_wide)
    hidden_fwd = smooth_gate(pre_fwd).astype(jnp.bfloat16)
    block_terms = jnp.einsum('thd,hkde->thke', hidden_fwd.astype(jnp.float32), weight_out_wide)
    ffn_fwd = jnp.zeros((TOK, DBLOCKS, BLOCK), jnp.float32).at[:, target_out].add(block_terms)
    out_acts = (forward_in.astype(jnp.float32) + ffn_fwd.reshape(TOK, D)).astype(jnp.bfloat16)
    picked_back = backward_in.reshape(TOK, DBLOCKS, BLOCK)[:, source_in]
    pre_back = jnp.einsum('thkc,hkcd->thd', picked_back.astype(jnp.float32), weight_in_wide)
    hidden_back = smooth_gate(pre_back).astype(jnp.bfloat16)
    grad_blocks = out_grad.reshape(TOK, DBLOCKS, BLOCK)[:, target_out]
    grad_hidden = jnp.einsum('thke,hkde->thd', grad_blocks.astype(jnp.float32), weight_out_wide)
    grad_pre = jax.vjp(smooth_gate, pre_back)[1](grad_hidden)[0].astype(jnp.bfloat16)
    grad_w_out = jnp.einsum('thd,thke->hkde', hidden_back.astype(jnp.float32), grad_blocks.astype(jnp.float32)).astype(jnp.bfloat16)
    grad_w_in = jnp.einsum('thkc,thd->hkcd', picked_back.astype(jnp.float32), grad_pre.astype(jnp.float32)).astype(jnp.bfloat16)
    back_terms = jnp.einsum('thd,hkcd->thkc', grad_pre.astype(jnp.float32), weight_in_wide)
    grad_input = jnp.zeros((TOK, DBLOCKS, BLOCK), jnp.float32).at[:, source_in].add(back_terms)
    in_grads = (out_grad.astype(jnp.float32) + grad_input.reshape(TOK, D)).astype(jnp.bfloat16)
    return (out_acts, in_grads, grad_w_in, grad_w_out)

def reference(handed_acts, handed_grads, saved_inputs, embedded, loss_grad, w_in, w_out, cols_in, cols_out):
    source_in = block_targets(cols_in)
    target_out = block_targets(cols_out)
    forward_all = jnp.concatenate([embedded[None], handed_acts[:-1]], axis=0)
    grads_all = jnp.concatenate([handed_grads[1:], loss_grad[None]], axis=0)

    def one_section(packed):
        return section_pass(packed[0], packed[1], packed[2], packed[3], packed[4], source_in, target_out)
    out_acts, in_grads, grad_w_in, grad_w_out = lax.map(one_section, (forward_all, saved_inputs, grads_all, w_in, w_out))
    return (out_acts, in_grads, grad_w_in, grad_w_out)
```

```python
import jax
import jax.numpy as jnp
from jax import lax
from jax.experimental import pallas as pl
from jax.experimental.pallas import tpu as pltpu
from jax.sharding import PartitionSpec as P

BF = jnp.bfloat16
F32 = jnp.float32
ROOT = 0.7978845608028654
CUBE = 0.044715


def dot(a, b, dims):
    return lax.dot_general(a, b, (dims, ((), ())), preferred_element_type=F32)


NN = ((1,), (0,))
NT = ((1,), (1,))
TN = ((0,), (0,))


def gelu(v):
    return 0.5 * v * (1.0 + jnp.tanh(ROOT * (v + CUBE * v * v * v)))


def gelu_and_slope(v):
    square = v * v
    t = jnp.tanh(ROOT * (v + CUBE * v * square))
    half = 0.5 * (1.0 + t)
    slope = half + 0.5 * v * (1.0 - t * t) * (ROOT * (1.0 + 3.0 * CUBE * square))
    return v * half, slope


def column(table, h, k, size):
    return pl.ds(pl.multiple_of(table[h, k] * size, size), size)


def picked(table, h, slots, size):
    return jnp.concatenate(
        [ref[:, column(table, h, k, size)] for k, ref in enumerate(slots)], axis=1
    )


def forward_kernel(cin, cout, x0, x1, x2, w_in, w_out, own, c1, c2, acc):
    h = pl.program_id(0)
    size = w_in.shape[-1]

    @pl.when(h == 0)
    def _():
        acc[0] = x0[...].astype(F32)
        acc[1] = jnp.zeros_like(acc[1])
        acc[2] = jnp.zeros_like(acc[2])

    x = picked(cin, h, (x0, x1, x2), size)
    pre = dot(x, w_in[0].reshape(3 * size, size), NN)
    hid = gelu(pre).astype(BF)
    for k in range(3):
        acc[k, :, column(cout, h, k, size)] += dot(hid, w_out[0, k], NN)

    @pl.when(h == pl.num_programs(0) - 1)
    def _():
        own[...] = acc[0]
        c1[...] = acc[1].astype(BF)
        c2[...] = acc[2].astype(BF)


def hidden_kernel(cin, x0, x1, x2, w_in, hid, slope):
    h = pl.program_id(0)
    size = w_in.shape[-1]
    x = picked(cin, h, (x0, x1, x2), size)
    pre = dot(x, w_in[0].reshape(3 * size, size), NN)
    value, rate = gelu_and_slope(pre)
    hid[...] = value.astype(BF)
    slope[...] = rate


def backward_kernel(cin, cout, g0, g1, g2, slope, w_in, w_out, own, c1, c2, dpre, acc):
    h = pl.program_id(0)
    size = w_in.shape[-1]

    @pl.when(h == 0)
    def _():
        acc[0] = g0[...].astype(F32)
        acc[1] = jnp.zeros_like(acc[1])
        acc[2] = jnp.zeros_like(acc[2])

    dhid = None
    for k, ref in enumerate((g0, g1, g2)):
        term = dot(ref[:, column(cout, h, k, size)], w_out[0, k], NT)
        dhid = term if dhid is None else dhid + term
    grad = (dhid * slope[...]).astype(BF)
    dpre[...] = grad
    for k in range(3):
        acc[k, :, column(cin, h, k, size)] += dot(grad, w_in[0, k], NT)

    @pl.when(h == pl.num_programs(0) - 1)
    def _():
        own[...] = acc[0]
        c1[...] = acc[1].astype(BF)
        c2[...] = acc[2].astype(BF)


def weights_kernel(cin, cout, x0, x1, x2, g0, g1, g2, hid, dpre, gw_in, gw_out):
    h = pl.program_id(0)
    size = gw_in.shape[-1]
    for k, (x, g) in enumerate(((x0, g0), (x1, g1), (x2, g2))):
        gw_out[0, k] = dot(hid[...], g[:, column(cout, h, k, size)], TN).astype(BF)
        gw_in[0, k] = dot(x[:, column(cin, h, k, size)], dpre[...], TN).astype(BF)


def whole(shape):
    return pl.BlockSpec(shape, lambda h, *_: (0,) * len(shape))


def run(body, tables, ins, in_specs, outs, out_specs, scratch, flops, name):
    size = sum(x.size * x.dtype.itemsize for x in ins) + sum(
        x.size * jnp.dtype(x.dtype).itemsize for x in outs
    )
    return pl.pallas_call(
        body,
        grid_spec=pltpu.PrefetchScalarGridSpec(
            num_scalar_prefetch=len(tables),
            grid=(tables[0].shape[0],),
            in_specs=in_specs,
            out_specs=out_specs,
            scratch_shapes=scratch,
        ),
        out_shape=outs,
        cost_estimate=pl.CostEstimate(flops=flops, bytes_accessed=size, transcendentals=0),
        name=name,
    )(*tables, *ins)


def shards(
    handed_acts, handed_grads, saved_inputs, embedded, loss_grad, w_in, w_out, cols_in, cols_out
):
    tokens, width = embedded.shape
    w_in, w_out = w_in[0], w_out[0]
    hidden, slots, size, _ = w_in.shape
    section = lax.axis_index("pipe")
    sections = lax.axis_size("pipe")
    group = lax.axis_size("tensor")
    masks = (0, 1, group // 2)

    def send(value, step, mask):
        route = [
            (s * group + t, (s + step) % sections * group + (t ^ mask))
            for s in range(sections)
            for t in range(group)
        ]
        return lax.ppermute(value, ("pipe", "tensor"), route)

    saved = saved_inputs[0]
    acts = jnp.where(section == sections - 1, embedded, handed_acts[0])
    grads = jnp.where(section == 0, loss_grad, handed_grads[0])
    xb = [saved] + [send(saved, 0, m) for m in masks[1:]]
    xa = [send(acts, 1, m) for m in masks]
    gb = [send(grads, -1, m) for m in masks]

    act = jax.ShapeDtypeStruct((tokens, width), BF)
    total = jax.ShapeDtypeStruct((tokens, width), F32)
    hid_bf = jax.ShapeDtypeStruct((tokens, hidden * size), BF)
    hid_f32 = jax.ShapeDtypeStruct((tokens, hidden * size), F32)
    weight = jax.ShapeDtypeStruct(w_in.shape, BF)
    act_spec = whole((tokens, width))
    hid_spec = pl.BlockSpec((tokens, size), lambda h, *_: (0, h))
    w_spec = pl.BlockSpec((1, slots, size, size), lambda h, *_: (h, 0, 0, 0))
    acc = pltpu.VMEM((slots, tokens, width), F32)
    unit = 2 * tokens * size * size * hidden * slots

    hid_b, slope_b = run(
        hidden_kernel, (cols_in,), (*xb, w_in), [act_spec] * 3 + [w_spec],
        (hid_bf, hid_f32), [hid_spec] * 2, [], unit, "hidden_b",
    )
    own_a, a1, a2 = run(
        forward_kernel, (cols_in, cols_out), (*xa, w_in, w_out), [act_spec] * 3 + [w_spec] * 2,
        (total, act, act), [act_spec] * 3, [acc], 2 * unit, "forward_a",
    )
    a1 = send(a1, 0, masks[1])
    a2 = send(a2, 0, masks[2])
    own_b, b1, b2, dpre = run(
        backward_kernel, (cols_in, cols_out), (*gb, slope_b, w_in, w_out),
        [act_spec] * 3 + [hid_spec] + [w_spec] * 2,
        (total, act, act, hid_bf), [act_spec] * 3 + [hid_spec], [acc], 2 * unit, "backward_b",
    )
    b1 = send(b1, 0, masks[1])
    b2 = send(b2, 0, masks[2])
    gw_in, gw_out = run(
        weights_kernel, (cols_in, cols_out), (*xb, *gb, hid_b, dpre),
        [act_spec] * 6 + [hid_spec] * 2, (weight, weight), [w_spec] * 2, [], 2 * unit, "weights_b",
    )
    out_acts = (own_a + a1.astype(F32) + a2.astype(F32)).astype(BF)
    in_grads = (own_b + b1.astype(F32) + b2.astype(F32)).astype(BF)
    return (out_acts[None], in_grads[None], gw_in[None], gw_out[None])


def solution(mesh):
    in_specs = (
        P("pipe", None, "tensor"),
        P("pipe", None, "tensor"),
        P("pipe", None, "tensor"),
        P(None, "tensor"),
        P(None, "tensor"),
        P("pipe", "tensor", None, None, None),
        P("pipe", "tensor", None, None, None),
        P("tensor", None),
        P("tensor", None),
    )
    out_specs = (
        P("pipe", None, "tensor"),
        P("pipe", None, "tensor"),
        P("pipe", "tensor", None, None, None),
        P("pipe", "tensor", None, None, None),
    )
    return jax.shard_map(shards, mesh=mesh, in_specs=in_specs, out_specs=out_specs, check_vma=False)
```

```python
import jax
import jax.numpy as jnp
from jax import lax
from jax.experimental import pallas as pl
from jax.experimental.pallas import tpu as pltpu
from jax.sharding import PartitionSpec as P

BF = jnp.bfloat16
F32 = jnp.float32
ROOT = 0.7978845608028654
CUBE = 0.044715


def dot(a, b, dims):
    return lax.dot_general(a, b, (dims, ((), ())), preferred_element_type=F32)


NN = ((1,), (0,))
NT = ((1,), (1,))
TN = ((0,), (0,))


def gelu(v):
    return 0.5 * v * (1.0 + jnp.tanh(ROOT * (v + CUBE * v * v * v)))


def gelu_and_slope(v):
    square = v * v
    t = jnp.tanh(ROOT * (v + CUBE * v * square))
    half = 0.5 * (1.0 + t)
    slope = half + 0.5 * v * (1.0 - t * t) * (ROOT * (1.0 + 3.0 * CUBE * square))
    return v * half, slope


def column(table, h, k, size):
    return pl.ds(pl.multiple_of(table[k, h] * size, size), size)


def picked(table, h, slots, size):
    return jnp.concatenate(
        [ref[:, column(table, h, k, size)] for k, ref in enumerate(slots)], axis=1
    )


def forward_kernel(cin, cout, x0, x1, x2, w_in, w_out, own, c1, c2, acc):
    hidden, slots, size, _ = w_in.shape
    own[...] = x0[...].astype(F32)
    acc[...] = jnp.zeros_like(acc)
    sums = (own, acc.at[0], acc.at[1])
    for h in range(hidden):
        x = picked(cin, h, (x0, x1, x2), size)
        pre = dot(x, w_in[h].reshape(slots * size, size), NN)
        hid = gelu(pre).astype(BF)
        for k in range(slots):
            sums[k][:, column(cout, h, k, size)] += dot(hid, w_out[h, k], NN)
    c1[...] = acc[0].astype(BF)
    c2[...] = acc[1].astype(BF)


def hidden_kernel(cin, x0, x1, x2, w_in, hid, slope):
    hidden, slots, size, _ = w_in.shape
    for h in range(hidden):
        x = picked(cin, h, (x0, x1, x2), size)
        pre = dot(x, w_in[h].reshape(slots * size, size), NN)
        value, rate = gelu_and_slope(pre)
        hid[:, h * size : (h + 1) * size] = value.astype(BF)
        slope[:, h * size : (h + 1) * size] = rate


def backward_kernel(cin, cout, g0, g1, g2, slope, w_in, w_out, own, c1, c2, dpre, acc):
    hidden, slots, size, _ = w_in.shape
    own[...] = g0[...].astype(F32)
    acc[...] = jnp.zeros_like(acc)
    sums = (own, acc.at[0], acc.at[1])
    for h in range(hidden):
        dhid = None
        for k, ref in enumerate((g0, g1, g2)):
            term = dot(ref[:, column(cout, h, k, size)], w_out[h, k], NT)
            dhid = term if dhid is None else dhid + term
        grad = (dhid * slope[:, h * size : (h + 1) * size]).astype(BF)
        dpre[:, h * size : (h + 1) * size] = grad
        for k in range(slots):
            sums[k][:, column(cin, h, k, size)] += dot(grad, w_in[h, k], NT)
    c1[...] = acc[0].astype(BF)
    c2[...] = acc[1].astype(BF)


def weights_kernel(
    cin, cout, x0, x1, x2, g0, g1, g2, hid, dpre, gw_in, gw_out, buf_in, buf_out, sems
):
    hidden, slots, size, _ = buf_in.shape
    copies = []
    for h in range(hidden):
        span = slice(h * size, (h + 1) * size)
        for k, (x, g) in enumerate(((x0, g0), (x1, g1), (x2, g2))):
            buf_out[h, k] = dot(hid[:, span], g[:, column(cout, h, k, size)], TN).astype(BF)
            buf_in[h, k] = dot(x[:, column(cin, h, k, size)], dpre[:, span], TN).astype(BF)
        for i, (src, dst) in enumerate(((buf_in, gw_in), (buf_out, gw_out))):
            copy = pltpu.make_async_copy(src.at[h], dst.at[h], sems.at[i, h])
            copy.start()
            copies.append(copy)
    for copy in copies:
        copy.wait()


VMEM = pl.BlockSpec(memory_space=pltpu.VMEM)
SMEM = pl.BlockSpec(memory_space=pltpu.SMEM)
ANY = pl.BlockSpec(memory_space=pl.ANY)


def run(body, tables, ins, outs, out_spec, scratch, flops, name):
    size = sum(x.size * x.dtype.itemsize for x in ins) + sum(
        x.size * jnp.dtype(x.dtype).itemsize for x in outs
    )
    return pl.pallas_call(
        body,
        in_specs=[SMEM] * len(tables) + [VMEM] * len(ins),
        out_specs=(out_spec,) * len(outs),
        scratch_shapes=scratch,
        out_shape=outs,
        cost_estimate=pl.CostEstimate(flops=flops, bytes_accessed=size, transcendentals=0),
        compiler_params=pltpu.CompilerParams(vmem_limit_bytes=16 << 20),
        name=name,
    )(*tables, *ins)


def shards(
    handed_acts, handed_grads, saved_inputs, embedded, loss_grad, w_in, w_out, cols_in, cols_out
):
    tokens, width = embedded.shape
    w_in, w_out = w_in[0], w_out[0]
    hidden, slots, size, _ = w_in.shape
    section = lax.axis_index("pipe")
    sections = lax.axis_size("pipe")
    group = lax.axis_size("tensor")
    masks = (0, 1, group // 2)

    def send(value, step, mask):
        route = [
            (s * group + t, (s + step) % sections * group + (t ^ mask))
            for s in range(sections)
            for t in range(group)
        ]
        return lax.ppermute(value, ("pipe", "tensor"), route)

    saved = saved_inputs[0]
    acts = jnp.where(section == sections - 1, embedded, handed_acts[0])
    grads = jnp.where(section == 0, loss_grad, handed_grads[0])
    xb = [saved] + [send(saved, 0, m) for m in masks[1:]]
    xa = [send(acts, 1, m) for m in masks]
    gb = [send(grads, -1, m) for m in masks]

    act = jax.ShapeDtypeStruct((tokens, width), BF)
    total = jax.ShapeDtypeStruct((tokens, width), F32)
    hid_bf = jax.ShapeDtypeStruct((tokens, hidden * size), BF)
    hid_f32 = jax.ShapeDtypeStruct((tokens, hidden * size), F32)
    weight = jax.ShapeDtypeStruct(w_in.shape, BF)
    acc = pltpu.VMEM((slots - 1, tokens, width), F32)
    unit = 2 * tokens * size * size * hidden * slots
    cin, cout = cols_in.T, cols_out.T

    hid_b, slope_b = run(
        hidden_kernel, (cin,), (*xb, w_in), (hid_bf, hid_f32), VMEM, [], unit, "hidden_b"
    )
    own_a, a1, a2 = run(
        forward_kernel, (cin, cout), (*xa, w_in, w_out), (total, act, act), VMEM, [acc],
        2 * unit, "forward_a",
    )
    a1 = send(a1, 0, masks[1])
    a2 = send(a2, 0, masks[2])
    own_b, b1, b2, dpre = run(
        backward_kernel, (cin, cout), (*gb, slope_b, w_in, w_out), (total, act, act, hid_bf),
        VMEM, [acc], 2 * unit, "backward_b",
    )
    b1 = send(b1, 0, masks[1])
    b2 = send(b2, 0, masks[2])
    stage = pltpu.VMEM(w_in.shape, BF)
    gw_in, gw_out = run(
        weights_kernel, (cin, cout), (*xb, *gb, hid_b, dpre), (weight, weight), ANY,
        [stage, stage, pltpu.SemaphoreType.DMA((2, hidden))], 2 * unit, "weights_b",
    )
    out_acts = (own_a + a1.astype(F32) + a2.astype(F32)).astype(BF)
    in_grads = (own_b + b1.astype(F32) + b2.astype(F32)).astype(BF)
    return (out_acts[None], in_grads[None], gw_in[None], gw_out[None])


def solution(mesh):
    in_specs = (
        P("pipe", None, "tensor"),
        P("pipe", None, "tensor"),
        P("pipe", None, "tensor"),
        P(None, "tensor"),
        P(None, "tensor"),
        P("pipe", "tensor", None, None, None),
        P("pipe", "tensor", None, None, None),
        P("tensor", None),
        P("tensor", None),
    )
    out_specs = (
        P("pipe", None, "tensor"),
        P("pipe", None, "tensor"),
        P("pipe", "tensor", None, None, None),
        P("pipe", "tensor", None, None, None),
    )
    return jax.shard_map(shards, mesh=mesh, in_specs=in_specs, out_specs=out_specs, check_vma=False)
```

```python
import functools

import jax
import jax.numpy as jnp
from jax import lax
from jax.experimental import pallas as pl
from jax.experimental.pallas import tpu as pltpu
from jax.sharding import PartitionSpec as P


BF = jnp.bfloat16
F32 = jnp.float32
ROOT = 0.7978845608028654
CUBE = 0.044715


def dot(a, b, dims):
    return lax.dot_general(a, b, (dims, ((), ())), preferred_element_type=F32)


NN = ((1,), (0,))
NT = ((1,), (1,))
TN = ((0,), (0,))


def gelu(v):
    return 0.5 * v * (1.0 + jnp.tanh(ROOT * (v + CUBE * v * v * v)))


def gelu_and_slope(v):
    square = v * v
    t = jnp.tanh(ROOT * (v + CUBE * v * square))
    half = 0.5 * (1.0 + t)
    slope = half + 0.5 * v * (1.0 - t * t) * (ROOT * (1.0 + 3.0 * CUBE * square))
    return v * half, slope


def column(table, h, k, size):
    return pl.ds(pl.multiple_of(table[k, h] * size, size), size)


def picked(table, h, slots, size):
    return jnp.concatenate(
        [ref[:, column(table, h, k, size)] for k, ref in enumerate(slots)], axis=1
    )


def forward_kernel(cin, cout, x0, x1, x2, w_in, w_out, own, c1, c2, acc):
    hidden, slots, size, _ = w_in.shape
    own[...] = x0[...].astype(F32)
    acc[...] = jnp.zeros_like(acc)
    sums = (own, acc.at[0], acc.at[1])
    for h in range(hidden):
        x = picked(cin, h, (x0, x1, x2), size)
        pre = dot(x, w_in[h].reshape(slots * size, size), NN)
        hid = gelu(pre).astype(BF)
        for k in range(slots):
            sums[k][:, column(cout, h, k, size)] += dot(hid, w_out[h, k], NN)
    c1[...] = acc[0].astype(BF)
    c2[...] = acc[1].astype(BF)


def hidden_kernel(cin, x0, x1, x2, w_in, hid, slope):
    hidden, slots, size, _ = w_in.shape
    for h in range(hidden):
        x = picked(cin, h, (x0, x1, x2), size)
        pre = dot(x, w_in[h].reshape(slots * size, size), NN)
        value, rate = gelu_and_slope(pre)
        hid[:, h * size : (h + 1) * size] = value.astype(BF)
        slope[:, h * size : (h + 1) * size] = rate


def backward_kernel(cin, cout, g0, g1, g2, slope, w_in, w_out, own, c1, c2, dpre, acc):
    hidden, slots, size, _ = w_in.shape
    own[...] = g0[...].astype(F32)
    acc[...] = jnp.zeros_like(acc)
    sums = (own, acc.at[0], acc.at[1])
    for h in range(hidden):
        dhid = None
        for k, ref in enumerate((g0, g1, g2)):
            term = dot(ref[:, column(cout, h, k, size)], w_out[h, k], NT)
            dhid = term if dhid is None else dhid + term
        grad = (dhid * slope[:, h * size : (h + 1) * size]).astype(BF)
        dpre[:, h * size : (h + 1) * size] = grad
        for k in range(slots):
            sums[k][:, column(cin, h, k, size)] += dot(grad, w_in[h, k], NT)
    c1[...] = acc[0].astype(BF)
    c2[...] = acc[1].astype(BF)


def weights_kernel(
    cin, cout, x0, x1, x2, g0, g1, g2, hid, dpre, gw_in, gw_out, buf_in, buf_out, sems
):
    hidden, _, size, _ = buf_in.shape
    copies = []
    for h in range(hidden):
        span = slice(h * size, (h + 1) * size)
        for k, (x, g) in enumerate(((x0, g0), (x1, g1), (x2, g2))):
            buf_out[h, k] = dot(hid[:, span], g[:, column(cout, h, k, size)], TN).astype(BF)
            buf_in[h, k] = dot(x[:, column(cin, h, k, size)], dpre[:, span], TN).astype(BF)
        for i, (src, dst) in enumerate(((buf_in, gw_in), (buf_out, gw_out))):
            copy = pltpu.make_async_copy(src.at[h], dst.at[h], sems.at[i, h])
            copy.start()
            copies.append(copy)
    for copy in copies:
        copy.wait()


VMEM = pl.BlockSpec(memory_space=pltpu.VMEM)
SMEM = pl.BlockSpec(memory_space=pltpu.SMEM)
HBM = pl.BlockSpec(memory_space=pltpu.HBM)


def in_hbm(*arrays):
    return [pltpu.with_memory_space_constraint(x, pltpu.HBM) for x in arrays]


def pick_kernel(
    sections, handed_a, first_a, handed_g, last_g, saved, cin, cout,
    acts, grads, kept, cin_v, cout_v, sems,
):
    section = lax.axis_index("pipe")
    ends = ((sections - 1, first_a, handed_a, acts), (0, last_g, handed_g, grads))
    fixed = ((cin, cin_v), (cout, cout_v), (saved, kept))
    copies = [pltpu.make_async_copy(*pair, sems.at[i]) for i, pair in enumerate(fixed)]

    def each(act):
        for i, (end, own, handed, out) in enumerate(ends):
            for src, hit in ((own, section == end), (handed, section != end)):

                @pl.when(hit)
                def _(src=src, out=out, i=i):
                    act(pltpu.make_async_copy(src, out, sems.at[len(fixed) + i]))

    each(lambda copy: copy.start())
    for copy in copies:
        copy.start()
    each(lambda copy: copy.wait())
    for copy in copies:
        copy.wait()


def pick(handed_a, first_a, handed_g, last_g, saved, cin, cout):
    act = jax.ShapeDtypeStruct(saved.shape, saved.dtype)
    table = jax.ShapeDtypeStruct(cin.shape, cin.dtype)
    return pl.pallas_call(
        functools.partial(pick_kernel, lax.axis_size("pipe")),
        in_specs=[HBM] * 7,
        out_specs=(VMEM,) * 5,
        scratch_shapes=[pltpu.SemaphoreType.DMA((5,))],
        out_shape=(act, act, act, table, table),
        cost_estimate=pl.CostEstimate(
            flops=0, bytes_accessed=6 * saved.size * saved.dtype.itemsize, transcendentals=0
        ),
        compiler_params=pltpu.CompilerParams(vmem_limit_bytes=4 << 20),
        name="pick",
    )(*in_hbm(handed_a, first_a, handed_g, last_g, saved, cin, cout))


def stage_kernel(w_in, w_out, w_in_v, w_out_v, sems):
    copies = [
        pltpu.make_async_copy(src.at[h], dst.at[h], sems.at[i, h])
        for i, (src, dst) in enumerate(((w_in, w_in_v), (w_out, w_out_v)))
        for h in range(src.shape[0])
    ]
    for copy in copies:
        copy.start()
    for copy in copies:
        copy.wait()


def stage(w_in, w_out):
    weight = jax.ShapeDtypeStruct(w_in.shape, w_in.dtype)
    return pl.pallas_call(
        stage_kernel,
        in_specs=[HBM] * 2,
        out_specs=(VMEM,) * 2,
        scratch_shapes=[pltpu.SemaphoreType.DMA((2, w_in.shape[0]))],
        out_shape=(weight, weight),
        cost_estimate=pl.CostEstimate(
            flops=0, bytes_accessed=4 * w_in.size * w_in.dtype.itemsize, transcendentals=0
        ),
        compiler_params=pltpu.CompilerParams(vmem_limit_bytes=8 << 20),
        name="stage",
    )(*in_hbm(w_in, w_out))


def run(body, tables, ins, outs, out_spec, scratch, flops):
    size = sum(x.size * x.dtype.itemsize for x in ins) + sum(
        x.size * jnp.dtype(x.dtype).itemsize for x in outs
    )
    return pl.pallas_call(
        body,
        in_specs=[SMEM] * len(tables) + [VMEM] * len(ins),
        out_specs=(out_spec,) * len(outs),
        scratch_shapes=scratch,
        out_shape=outs,
        cost_estimate=pl.CostEstimate(flops=flops, bytes_accessed=size, transcendentals=0),
        compiler_params=pltpu.CompilerParams(vmem_limit_bytes=16 << 20),
    )(*tables, *ins)


def shards(
    handed_acts, handed_grads, saved_inputs, embedded, loss_grad, w_in, w_out, cols_in, cols_out
):
    tokens, width = embedded.shape
    w_in, w_out = w_in[0], w_out[0]
    hidden, slots, size, _ = w_in.shape
    sections = lax.axis_size("pipe")
    group = lax.axis_size("tensor")
    masks = (0, 1, group // 2)

    def send(value, step, mask):
        route = [
            (s * group + t, (s + step) % sections * group + (t ^ mask))
            for s in range(sections)
            for t in range(group)
        ]
        return lax.ppermute(value, ("pipe", "tensor"), route)

    def exchange(values, step=0):
        got = []
        for k in (1, 2):
            value = values[k - 1] if isinstance(values, tuple) else values
            got.append(send(value, step, masks[k]))
        return got

    saved = saved_inputs[0]
    xb = [saved] + exchange(saved)
    acts, grads, kept, cin, cout = pick(
        handed_acts[0], embedded, handed_grads[0], loss_grad, saved, cols_in.T, cols_out.T
    )
    xb[0] = kept
    far = exchange(acts, step=1)
    xa = [send(acts, 1, 0)] + far
    grads = send(grads, -1, 0)
    w_in, w_out = stage(w_in, w_out)
    gb = [grads] + exchange(grads)

    act = jax.ShapeDtypeStruct((tokens, width), BF)
    total = jax.ShapeDtypeStruct((tokens, width), F32)
    hid_bf = jax.ShapeDtypeStruct((tokens, hidden * size), BF)
    hid_f32 = jax.ShapeDtypeStruct((tokens, hidden * size), F32)
    weight = jax.ShapeDtypeStruct(w_in.shape, BF)
    acc = pltpu.VMEM((slots - 1, tokens, width), F32)
    unit = 2 * tokens * size * size * hidden * slots

    hid_b, slope_b = run(hidden_kernel, (cin,), (*xb, w_in), (hid_bf, hid_f32), VMEM, [], unit)
    own_a, a1, a2 = run(
        forward_kernel, (cin, cout), (*xa, w_in, w_out), (total, act, act), VMEM, [acc],
        2 * unit,
    )
    a1, a2 = exchange((a1, a2))
    own_b, b1, b2, dpre = run(
        backward_kernel, (cin, cout), (*gb, slope_b, w_in, w_out), (total, act, act, hid_bf),
        VMEM, [acc], 2 * unit,
    )
    b1, b2 = exchange((b1, b2))
    held = pltpu.VMEM(w_in.shape, BF)
    gw_in, gw_out = run(
        weights_kernel, (cin, cout), (*xb, *gb, hid_b, dpre), (weight, weight), HBM,
        [held, held, pltpu.SemaphoreType.DMA((2, hidden))], 2 * unit,
    )
    out_acts = (own_a + a1.astype(F32) + a2.astype(F32)).astype(BF)
    in_grads = (own_b + b1.astype(F32) + b2.astype(F32)).astype(BF)
    return (out_acts[None], in_grads[None], gw_in[None], gw_out[None])


def solution(mesh):
    in_specs = (
        P("pipe", None, "tensor"),
        P("pipe", None, "tensor"),
        P("pipe", None, "tensor"),
        P(None, "tensor"),
        P(None, "tensor"),
        P("pipe", "tensor", None, None, None),
        P("pipe", "tensor", None, None, None),
        P("tensor", None),
        P("tensor", None),
    )
    out_specs = (
        P("pipe", None, "tensor"),
        P("pipe", None, "tensor"),
        P("pipe", "tensor", None, None, None),
        P("pipe", "tensor", None, None, None),
    )
    return jax.shard_map(shards, mesh=mesh, in_specs=in_specs, out_specs=out_specs, check_vma=False)
```

```python
import functools

import jax
import jax.numpy as jnp
from jax import lax
from jax.experimental import pallas as pl
from jax.experimental.pallas import tpu as pltpu
from jax.sharding import PartitionSpec as P


BF = jnp.bfloat16
F32 = jnp.float32
ROOT = 0.7978845608028654
CUBE = 0.044715


def dot(a, b, dims):
    return lax.dot_general(a, b, (dims, ((), ())), preferred_element_type=F32)


NN = ((1,), (0,))
NT = ((1,), (1,))
TN = ((0,), (0,))


def gelu(v):
    return 0.5 * v * (1.0 + jnp.tanh(ROOT * (v + CUBE * v * v * v)))


def gelu_and_slope(v):
    square = v * v
    t = jnp.tanh(ROOT * (v + CUBE * v * square))
    half = 0.5 * (1.0 + t)
    slope = half + 0.5 * v * (1.0 - t * t) * (ROOT * (1.0 + 3.0 * CUBE * square))
    return v * half, slope


def column(table, h, k, size):
    return pl.ds(pl.multiple_of(table[k, h] * size, size), size)


def picked(table, h, slots, size):
    return jnp.concatenate(
        [ref[:, column(table, h, k, size)] for k, ref in enumerate(slots)], axis=1
    )


def forward_kernel(cin, cout, x0, x1, x2, w_in, w_out, own, c1, c2, acc):
    hidden, slots, size, _ = w_in.shape
    own[...] = x0[...].astype(F32)
    acc[...] = jnp.zeros_like(acc)
    sums = (own, acc.at[0], acc.at[1])
    for h in range(hidden):
        x = picked(cin, h, (x0, x1, x2), size)
        pre = dot(x, w_in[h].reshape(slots * size, size), NN)
        hid = gelu(pre).astype(BF)
        for k in range(slots):
            sums[k][:, column(cout, h, k, size)] += dot(hid, w_out[h, k], NN)
    c1[...] = acc[0].astype(BF)
    c2[...] = acc[1].astype(BF)


def hidden_kernel(cin, x0, x1, x2, w_in, hid, slope):
    hidden, slots, size, _ = w_in.shape
    for h in range(hidden):
        x = picked(cin, h, (x0, x1, x2), size)
        pre = dot(x, w_in[h].reshape(slots * size, size), NN)
        value, rate = gelu_and_slope(pre)
        hid[:, h * size : (h + 1) * size] = value.astype(BF)
        slope[:, h * size : (h + 1) * size] = rate


def backward_kernel(
    cin, cout, g0, g1, g2, slope, w_in, w_out, own, c1_top, c2_top, c1_low, c2_low, dpre, acc
):
    hidden, slots, size, _ = w_in.shape
    own[...] = g0[...].astype(F32)
    acc[...] = jnp.zeros_like(acc)
    sums = (own, acc.at[0], acc.at[1])
    for h in range(hidden):
        dhid = None
        for k, ref in enumerate((g0, g1, g2)):
            term = dot(ref[:, column(cout, h, k, size)], w_out[h, k], NT)
            dhid = term if dhid is None else dhid + term
        grad = (dhid * slope[:, h * size : (h + 1) * size]).astype(BF)
        dpre[:, h * size : (h + 1) * size] = grad
        for k in range(slots):
            sums[k][:, column(cin, h, k, size)] += dot(grad, w_in[h, k], NT)
    top = c1_top.shape[0]
    c1_top[...] = acc[0, :top].astype(BF)
    c2_top[...] = acc[1, :top].astype(BF)
    c1_low[...] = acc[0, top:].astype(BF)
    c2_low[...] = acc[1, top:].astype(BF)


def weights_kernel(
    cin, cout, x0, x1, x2, g0, g1, g2, hid, dpre, gw_in, gw_out, buf_in, buf_out, sems
):
    hidden, _, size, _ = buf_in.shape
    copies = []
    for h in range(hidden):
        span = slice(h * size, (h + 1) * size)
        for k, (x, g) in enumerate(((x0, g0), (x1, g1), (x2, g2))):
            buf_out[h, k] = dot(hid[:, span], g[:, column(cout, h, k, size)], TN).astype(BF)
            buf_in[h, k] = dot(x[:, column(cin, h, k, size)], dpre[:, span], TN).astype(BF)
        for i, (src, dst) in enumerate(((buf_in, gw_in), (buf_out, gw_out))):
            copy = pltpu.make_async_copy(src.at[h], dst.at[h], sems.at[i, h])
            copy.start()
            copies.append(copy)
    for copy in copies:
        copy.wait()


VMEM = pl.BlockSpec(memory_space=pltpu.VMEM)
SMEM = pl.BlockSpec(memory_space=pltpu.SMEM)
HBM = pl.BlockSpec(memory_space=pltpu.HBM)


def in_hbm(*arrays):
    return [pltpu.with_memory_space_constraint(x, pltpu.HBM) for x in arrays]


def pick_kernel(
    sections, handed_a, first_a, handed_g, last_g, saved, cin, cout,
    acts, grads, kept, cin_v, cout_v, sems,
):
    section = lax.axis_index("pipe")
    ends = ((sections - 1, first_a, handed_a, acts), (0, last_g, handed_g, grads))
    fixed = ((cin, cin_v), (cout, cout_v), (saved, kept))
    copies = [pltpu.make_async_copy(*pair, sems.at[i]) for i, pair in enumerate(fixed)]

    def each(act):
        for i, (end, own, handed, out) in enumerate(ends):
            for src, hit in ((own, section == end), (handed, section != end)):

                @pl.when(hit)
                def _(src=src, out=out, i=i):
                    act(pltpu.make_async_copy(src, out, sems.at[len(fixed) + i]))

    each(lambda copy: copy.start())
    for copy in copies:
        copy.start()
    each(lambda copy: copy.wait())
    for copy in copies:
        copy.wait()


def pick(handed_a, first_a, handed_g, last_g, saved, cin, cout):
    act = jax.ShapeDtypeStruct(saved.shape, saved.dtype)
    table = jax.ShapeDtypeStruct(cin.shape, cin.dtype)
    return pl.pallas_call(
        functools.partial(pick_kernel, lax.axis_size("pipe")),
        in_specs=[HBM] * 7,
        out_specs=(VMEM,) * 5,
        scratch_shapes=[pltpu.SemaphoreType.DMA((5,))],
        out_shape=(act, act, act, table, table),
        cost_estimate=pl.CostEstimate(
            flops=0, bytes_accessed=6 * saved.size * saved.dtype.itemsize, transcendentals=0
        ),
        compiler_params=pltpu.CompilerParams(vmem_limit_bytes=4 << 20),
        name="pick",
    )(*in_hbm(handed_a, first_a, handed_g, last_g, saved, cin, cout))


def stage_kernel(w_in, w_out, w_in_v, w_out_v, sems):
    copies = [
        pltpu.make_async_copy(src.at[h], dst.at[h], sems.at[i, h])
        for i, (src, dst) in enumerate(((w_in, w_in_v), (w_out, w_out_v)))
        for h in range(src.shape[0])
    ]
    for copy in copies:
        copy.start()
    for copy in copies:
        copy.wait()


def stage(w_in, w_out):
    weight = jax.ShapeDtypeStruct(w_in.shape, w_in.dtype)
    return pl.pallas_call(
        stage_kernel,
        in_specs=[HBM] * 2,
        out_specs=(VMEM,) * 2,
        scratch_shapes=[pltpu.SemaphoreType.DMA((2, w_in.shape[0]))],
        out_shape=(weight, weight),
        cost_estimate=pl.CostEstimate(
            flops=0, bytes_accessed=4 * w_in.size * w_in.dtype.itemsize, transcendentals=0
        ),
        compiler_params=pltpu.CompilerParams(vmem_limit_bytes=8 << 20),
        name="stage",
    )(*in_hbm(w_in, w_out))


def finish_kernel(first, own, c1, c2, *rest):
    out, buf, sem = rest[-3:]
    rows = pl.ds(first, c1.shape[0])
    buf[...] = (own[rows, :] + c1[...].astype(F32) + c2[...].astype(F32)).astype(BF)
    copy = pltpu.make_async_copy(buf, out.at[rows, :], sem)
    copy.start()
    copy.wait()


def finish(first, own, c1, c2, begun=()):
    return pl.pallas_call(
        functools.partial(finish_kernel, first),
        in_specs=[VMEM] * 3 + [HBM] * len(begun),
        out_specs=HBM,
        scratch_shapes=[pltpu.VMEM(c1.shape, BF), pltpu.SemaphoreType.DMA],
        out_shape=jax.ShapeDtypeStruct(own.shape, BF),
        input_output_aliases={3: 0} if begun else {},
        cost_estimate=pl.CostEstimate(
            flops=2 * c1.size, bytes_accessed=10 * c1.size, transcendentals=0
        ),
        compiler_params=pltpu.CompilerParams(vmem_limit_bytes=4 << 20),
        name="finish",
    )(own, c1, c2, *begun)


def run(body, tables, ins, outs, out_spec, scratch, flops):
    size = sum(x.size * x.dtype.itemsize for x in ins) + sum(
        x.size * jnp.dtype(x.dtype).itemsize for x in outs
    )
    return pl.pallas_call(
        body,
        in_specs=[SMEM] * len(tables) + [VMEM] * len(ins),
        out_specs=(out_spec,) * len(outs),
        scratch_shapes=scratch,
        out_shape=outs,
        cost_estimate=pl.CostEstimate(flops=flops, bytes_accessed=size, transcendentals=0),
        compiler_params=pltpu.CompilerParams(vmem_limit_bytes=16 << 20),
    )(*tables, *ins)


def shards(
    handed_acts, handed_grads, saved_inputs, embedded, loss_grad, w_in, w_out, cols_in, cols_out
):
    tokens, width = embedded.shape
    w_in, w_out = w_in[0], w_out[0]
    hidden, slots, size, _ = w_in.shape
    sections = lax.axis_size("pipe")
    group = lax.axis_size("tensor")
    masks = (0, 1, group // 2)

    def send(value, step, mask):
        route = [
            (s * group + t, (s + step) % sections * group + (t ^ mask))
            for s in range(sections)
            for t in range(group)
        ]
        return lax.ppermute(value, ("pipe", "tensor"), route)

    def exchange(values, step=0):
        got = []
        for k in (1, 2):
            value = values[k - 1] if isinstance(values, tuple) else values
            got.append(send(value, step, masks[k]))
        return got

    saved = saved_inputs[0]
    xb = [saved] + exchange(saved)
    acts, grads, kept, cin, cout = pick(
        handed_acts[0], embedded, handed_grads[0], loss_grad, saved, cols_in.T, cols_out.T
    )
    xb[0] = kept
    far = exchange(acts, step=1)
    xa = [send(acts, 1, 0)] + far
    grads = send(grads, -1, 0)
    w_in, w_out = stage(w_in, w_out)
    gb = [grads] + exchange(grads)

    act = jax.ShapeDtypeStruct((tokens, width), BF)
    total = jax.ShapeDtypeStruct((tokens, width), F32)
    hid_bf = jax.ShapeDtypeStruct((tokens, hidden * size), BF)
    hid_f32 = jax.ShapeDtypeStruct((tokens, hidden * size), F32)
    weight = jax.ShapeDtypeStruct(w_in.shape, BF)
    acc = pltpu.VMEM((slots - 1, tokens, width), F32)
    unit = 2 * tokens * size * size * hidden * slots

    hid_b, slope_b = run(hidden_kernel, (cin,), (*xb, w_in), (hid_bf, hid_f32), VMEM, [], unit)
    own_a, a1, a2 = run(
        forward_kernel, (cin, cout), (*xa, w_in, w_out), (total, act, act), VMEM, [acc],
        2 * unit,
    )
    a1, a2 = exchange((a1, a2))
    cut = tokens - tokens // 4
    top = jax.ShapeDtypeStruct((cut, width), BF)
    low = jax.ShapeDtypeStruct((tokens - cut, width), BF)
    own_b, b1, b2, b1_low, b2_low, dpre = run(
        backward_kernel, (cin, cout), (*gb, slope_b, w_in, w_out),
        (total, top, top, low, low, hid_bf), VMEM, [acc], 2 * unit,
    )
    b1, b2 = exchange((b1, b2))
    b1_low, b2_low = exchange((b1_low, b2_low))
    held = pltpu.VMEM(w_in.shape, BF)
    gw_in, gw_out = run(
        weights_kernel, (cin, cout), (*xb, *gb, hid_b, dpre), (weight, weight), HBM,
        [held, held, pltpu.SemaphoreType.DMA((2, hidden))], 2 * unit,
    )
    out_acts = (own_a + a1.astype(F32) + a2.astype(F32)).astype(BF)
    in_grads = finish(0, own_b, b1, b2)
    in_grads = finish(cut, own_b, b1_low, b2_low, (in_grads,))
    return (out_acts[None], in_grads[None], gw_in[None], gw_out[None])


def solution(mesh):
    in_specs = (
        P("pipe", None, "tensor"),
        P("pipe", None, "tensor"),
        P("pipe", None, "tensor"),
        P(None, "tensor"),
        P(None, "tensor"),
        P("pipe", "tensor", None, None, None),
        P("pipe", "tensor", None, None, None),
        P("tensor", None),
        P("tensor", None),
    )
    out_specs = (
        P("pipe", None, "tensor"),
        P("pipe", None, "tensor"),
        P("pipe", "tensor", None, None, None),
        P("pipe", "tensor", None, None, None),
    )
    return jax.shard_map(shards, mesh=mesh, in_specs=in_specs, out_specs=out_specs, check_vma=False)
```

```python
import functools

import jax
import jax.numpy as jnp
from jax import lax
from jax.experimental import pallas as pl
from jax.experimental.pallas import tpu as pltpu
from jax.sharding import PartitionSpec as P


BF = jnp.bfloat16
F32 = jnp.float32
ROOT = 0.7978845608028654
CUBE = 0.044715


def dot(a, b, dims):
    return lax.dot_general(a, b, (dims, ((), ())), preferred_element_type=F32)


NN = ((1,), (0,))
NT = ((1,), (1,))
TN = ((0,), (0,))


def gelu(v):
    half = 0.5 * v
    return half + half * jnp.tanh(v * (ROOT + (ROOT * CUBE) * (v * v)))


def gelu_and_slope(v):
    square = v * v
    t = jnp.tanh(ROOT * (v + CUBE * v * square))
    half = 0.5 * (1.0 + t)
    slope = half + 0.5 * v * (1.0 - t * t) * (ROOT * (1.0 + 3.0 * CUBE * square))
    return v * half, slope


def column(table, h, k, size):
    return pl.ds(pl.multiple_of(table[k, h] * size, size), size)


def picked(table, h, slots, size):
    return jnp.concatenate(
        [ref[:, column(table, h, k, size)] for k, ref in enumerate(slots)], axis=1
    )


def forward_kernel(cin, cout, x0, x1, x2, w_in, w_out, own, c1, c2, acc):
    hidden, slots, size, _ = w_in.shape
    sums = (own, acc.at[0], acc.at[1])

    def value(h):
        x = picked(cin, h, (x0, x1, x2), size)
        return dot(x, w_in[h].reshape(slots * size, size), NN)

    pre = value(0)
    own[...] = x0[...].astype(F32)
    acc[...] = jnp.zeros_like(acc)
    for h in range(hidden):
        later = value(h + 1) if h + 1 < hidden else None
        hid = gelu(pre).astype(BF)
        for k in range(slots):
            sums[k][:, column(cout, h, k, size)] += dot(hid, w_out[h, k], NN)
        pre = later
    c1[...] = acc[0].astype(BF)
    c2[...] = acc[1].astype(BF)


def hidden_kernel(cin, x0, x1, x2, w_in, hid, slope):
    hidden, slots, size, _ = w_in.shape
    for h in range(hidden):
        x = picked(cin, h, (x0, x1, x2), size)
        pre = dot(x, w_in[h].reshape(slots * size, size), NN)
        value, rate = gelu_and_slope(pre)
        hid[:, h * size : (h + 1) * size] = value.astype(BF)
        slope[:, h * size : (h + 1) * size] = rate


def backward_kernel(cin, cout, g0, g1, g2, slope, w_in, w_out, own, c1, c2, dpre, acc):
    hidden, slots, size, _ = w_in.shape
    own[...] = g0[...].astype(F32)
    acc[...] = jnp.zeros_like(acc)
    sums = (own, acc.at[0], acc.at[1])
    for h in range(hidden):
        dhid = None
        for k, ref in enumerate((g0, g1, g2)):
            term = dot(ref[:, column(cout, h, k, size)], w_out[h, k], NT)
            dhid = term if dhid is None else dhid + term
        grad = (dhid * slope[:, h * size : (h + 1) * size]).astype(BF)
        dpre[:, h * size : (h + 1) * size] = grad
        for k in range(slots):
            sums[k][:, column(cin, h, k, size)] += dot(grad, w_in[h, k], NT)
    c1[...] = acc[0].astype(BF)
    c2[...] = acc[1].astype(BF)


def weights_kernel(
    cin, cout, x0, x1, x2, g0, g1, g2, hid, dpre, gw_in, gw_out, buf_in, buf_out, sems
):
    hidden, _, size, _ = buf_in.shape
    copies = []
    for h in range(hidden):
        span = slice(h * size, (h + 1) * size)
        for k, (x, g) in enumerate(((x0, g0), (x1, g1), (x2, g2))):
            buf_out[h, k] = dot(hid[:, span], g[:, column(cout, h, k, size)], TN).astype(BF)
            buf_in[h, k] = dot(x[:, column(cin, h, k, size)], dpre[:, span], TN).astype(BF)
        for i, (src, dst) in enumerate(((buf_in, gw_in), (buf_out, gw_out))):
            copy = pltpu.make_async_copy(src.at[h], dst.at[h], sems.at[i, h])
            copy.start()
            copies.append(copy)
    for copy in copies:
        copy.wait()


VMEM = pl.BlockSpec(memory_space=pltpu.VMEM)
SMEM = pl.BlockSpec(memory_space=pltpu.SMEM)
HBM = pl.BlockSpec(memory_space=pltpu.HBM)


def in_hbm(*arrays):
    return [pltpu.with_memory_space_constraint(x, pltpu.HBM) for x in arrays]


def pick_kernel(
    sections, handed_a, first_a, handed_g, last_g, saved, cin, cout,
    acts, grads, kept, cin_v, cout_v, sems,
):
    section = lax.axis_index("pipe")
    ends = ((sections - 1, first_a, handed_a, acts), (0, last_g, handed_g, grads))
    fixed = ((cin, cin_v), (cout, cout_v), (saved, kept))
    copies = [pltpu.make_async_copy(*pair, sems.at[i]) for i, pair in enumerate(fixed)]

    def each(act):
        for i, (end, own, handed, out) in enumerate(ends):
            for src, hit in ((own, section == end), (handed, section != end)):

                @pl.when(hit)
                def _(src=src, out=out, i=i):
                    act(pltpu.make_async_copy(src, out, sems.at[len(fixed) + i]))

    each(lambda copy: copy.start())
    for copy in copies:
        copy.start()
    each(lambda copy: copy.wait())
    for copy in copies:
        copy.wait()


def pick(handed_a, first_a, handed_g, last_g, saved, cin, cout):
    act = jax.ShapeDtypeStruct(saved.shape, saved.dtype)
    table = jax.ShapeDtypeStruct(cin.shape, cin.dtype)
    return pl.pallas_call(
        functools.partial(pick_kernel, lax.axis_size("pipe")),
        in_specs=[HBM] * 7,
        out_specs=(VMEM,) * 5,
        scratch_shapes=[pltpu.SemaphoreType.DMA((5,))],
        out_shape=(act, act, act, table, table),
        cost_estimate=pl.CostEstimate(
            flops=0, bytes_accessed=6 * saved.size * saved.dtype.itemsize, transcendentals=0
        ),
        compiler_params=pltpu.CompilerParams(vmem_limit_bytes=4 << 20),
        name="pick",
    )(*in_hbm(handed_a, first_a, handed_g, last_g, saved, cin, cout))


def stage_kernel(w_in, w_out, w_in_v, w_out_v, sems):
    copies = [
        pltpu.make_async_copy(src.at[h], dst.at[h], sems.at[i, h])
        for i, (src, dst) in enumerate(((w_in, w_in_v), (w_out, w_out_v)))
        for h in range(src.shape[0])
    ]
    for copy in copies:
        copy.start()
    for copy in copies:
        copy.wait()


def stage(w_in, w_out):
    weight = jax.ShapeDtypeStruct(w_in.shape, w_in.dtype)
    return pl.pallas_call(
        stage_kernel,
        in_specs=[HBM] * 2,
        out_specs=(VMEM,) * 2,
        scratch_shapes=[pltpu.SemaphoreType.DMA((2, w_in.shape[0]))],
        out_shape=(weight, weight),
        cost_estimate=pl.CostEstimate(
            flops=0, bytes_accessed=4 * w_in.size * w_in.dtype.itemsize, transcendentals=0
        ),
        compiler_params=pltpu.CompilerParams(vmem_limit_bytes=8 << 20),
        name="stage",
    )(*in_hbm(w_in, w_out))


def run(body, tables, ins, outs, out_spec, scratch, flops):
    size = sum(x.size * x.dtype.itemsize for x in ins) + sum(
        x.size * jnp.dtype(x.dtype).itemsize for x in outs
    )
    return pl.pallas_call(
        body,
        in_specs=[SMEM] * len(tables) + [VMEM] * len(ins),
        out_specs=(out_spec,) * len(outs),
        scratch_shapes=scratch,
        out_shape=outs,
        cost_estimate=pl.CostEstimate(flops=flops, bytes_accessed=size, transcendentals=0),
        compiler_params=pltpu.CompilerParams(vmem_limit_bytes=16 << 20),
    )(*tables, *ins)


def shards(
    handed_acts, handed_grads, saved_inputs, embedded, loss_grad, w_in, w_out, cols_in, cols_out
):
    tokens, width = embedded.shape
    w_in, w_out = w_in[0], w_out[0]
    hidden, slots, size, _ = w_in.shape
    sections = lax.axis_size("pipe")
    group = lax.axis_size("tensor")
    masks = (0, 1, group // 2)

    def send(value, step, mask):
        route = [
            (s * group + t, (s + step) % sections * group + (t ^ mask))
            for s in range(sections)
            for t in range(group)
        ]
        return lax.ppermute(value, ("pipe", "tensor"), route)

    def exchange(values, step=0):
        got = []
        for k in (1, 2):
            value = values[k - 1] if isinstance(values, tuple) else values
            got.append(send(value, step, masks[k]))
        return got

    saved = saved_inputs[0]
    xb = [saved] + exchange(saved)
    acts, grads, kept, cin, cout = pick(
        handed_acts[0], embedded, handed_grads[0], loss_grad, saved, cols_in.T, cols_out.T
    )
    xb[0] = kept
    far = exchange(acts, step=1)
    xa = [send(acts, 1, 0)] + far
    grads = send(grads, -1, 0)
    w_in, w_out = stage(w_in, w_out)
    gb = [grads] + exchange(grads)

    act = jax.ShapeDtypeStruct((tokens, width), BF)
    total = jax.ShapeDtypeStruct((tokens, width), F32)
    hid_bf = jax.ShapeDtypeStruct((tokens, hidden * size), BF)
    hid_f32 = jax.ShapeDtypeStruct((tokens, hidden * size), F32)
    weight = jax.ShapeDtypeStruct(w_in.shape, BF)
    acc = pltpu.VMEM((slots - 1, tokens, width), F32)
    unit = 2 * tokens * size * size * hidden * slots

    hid_b, slope_b = run(hidden_kernel, (cin,), (*xb, w_in), (hid_bf, hid_f32), VMEM, [], unit)
    own_a, a1, a2 = run(
        forward_kernel, (cin, cout), (*xa, w_in, w_out), (total, act, act), VMEM, [acc],
        2 * unit,
    )
    a1, a2 = exchange((a1, a2))
    own_b, b1, b2, dpre = run(
        backward_kernel, (cin, cout), (*gb, slope_b, w_in, w_out), (total, act, act, hid_bf),
        VMEM, [acc], 2 * unit,
    )
    b1, b2 = exchange((b1, b2))
    held = pltpu.VMEM(w_in.shape, BF)
    gw_in, gw_out = run(
        weights_kernel, (cin, cout), (*xb, *gb, hid_b, dpre), (weight, weight), HBM,
        [held, held, pltpu.SemaphoreType.DMA((2, hidden))], 2 * unit,
    )
    out_acts = (own_a + a1.astype(F32) + a2.astype(F32)).astype(BF)
    in_grads = (own_b + b1.astype(F32) + b2.astype(F32)).astype(BF)
    return (out_acts[None], in_grads[None], gw_in[None], gw_out[None])


def solution(mesh):
    in_specs = (
        P("pipe", None, "tensor"),
        P("pipe", None, "tensor"),
        P("pipe", None, "tensor"),
        P(None, "tensor"),
        P(None, "tensor"),
        P("pipe", "tensor", None, None, None),
        P("pipe", "tensor", None, None, None),
        P("tensor", None),
        P("tensor", None),
    )
    out_specs = (
        P("pipe", None, "tensor"),
        P("pipe", None, "tensor"),
        P("pipe", "tensor", None, None, None),
        P("pipe", "tensor", None, None, None),
    )
    return jax.shard_map(shards, mesh=mesh, in_specs=in_specs, out_specs=out_specs, check_vma=False)
```
